32 devices in a mesh: groups: 2 (over y), dp: 4 (over z), mp: 2 (over x), layer: 2 (over core).
Axes of the slice: x: 2, y: 2, z: 4, core: 2. Of those that a mesh axis runs over, the one named last changes fastest.
Arguments:
- acts: bfloat16 [2, 4096, 8192], P('layer', ('groups', 'dp'), 'mp'), parts along dimension 1, may hold values from -6 to 6
- grads: bfloat16 [2, 4096, 28672], P('layer', ('groups', 'dp'), 'mp'), parts along dimension 1, may hold values from -6 to 6
- query_left: bfloat16 [2, 8192, 512], P('layer', ('mp', 'dp'), 'groups'), parts along dimension 2, may hold values from -0.0625 to 0.0625
- query_right: bfloat16 [2, 28672, 512], P('layer', ('mp', 'dp'), 'groups'), parts along dimension 2, may hold values from -0.03125 to 0.03125
- seq_len: int32 [16], P(('groups', 'dp')), parts along dimension 0, may hold values from 1 to 256, 1024 in all
Outputs:
- scores: float32 [2, 16, 32], P('layer', ('groups', 'dp')), parts along dimension 1
The draws below stay inside these ranges and needn't reach their ends.
There are 2 independent parts, one for each index of `groups`. The reference program is written for one: setup_inputs(seed, part) draws one part's arguments, and reference() takes and returns one part's arrays. A program takes and returns all parts, laid end to end along the dimension named above; each array names one. Nothing has to cross between parts.
Inputs may be any that keep to these rules, and one draw needn't show every extreme that they name: `seq_len`: every sequence has at least one live token and some sequence has exactly 256.
All inputs are finite; a program needn't handle non-finite values. No bound on the sum of `seq_len` on one device may be relied on, other than what follows from the above.
Results may differ from the reference program's by a relative error of at most 0.0003.
Values may be sent and summed in bfloat16 or wider, within the bound.
A program may use at most 64 MiB of HBM per device.

```python
import math
import jax
import jax.numpy as jnp
import numpy as np
from jax import lax

D = 8192
F = 28672
NQ = 32
RANK = 8
LAYERS = 2
LEN = 256
SEQS = 8
TOKENS = 2048
QR = 256


def levels(rng, dims, cuts, low, high):
    def one(axis_at, blocks):
        steps = jax.random.uniform(jax.random.fold_in(jax.random.fold_in(rng, 6), axis_at), (blocks,), jnp.float32, low / len(cuts), high / len(cuts))
        return jnp.repeat(jnp.exp(steps), dims[axis_at] // blocks).reshape((-1,) + (1,) * (len(dims) - axis_at - 1))

    level = one(*cuts[0])
    for cut in cuts[1:]:
        level = level * one(*cut)
    return level


def profile(number_of, total, reach, lean):
    loads = [(1 << 20) // math.isqrt(standing ** lean) + 1 for standing in range(2, number_of + 1)]
    rest, holding = total - reach - (number_of - 1), [1] * (number_of - 1)
    while rest > 0:
        free = [i for i in range(number_of - 1) if holding[i] < reach]
        mass, left = sum([loads[i] for i in free]), rest
        for i in free:
            more = min(reach - holding[i], max(1, left * loads[i] // mass), rest)
            holding[i] = holding[i] + more
            rest = rest - more
    return np.array([reach] + holding)


def uneven(rng, number_of, total, limit, skew):
    if number_of == 2:
        one = jax.random.randint(rng, (), max(1, total - limit), min(limit, total - 1) + 1)
        return jnp.stack([one, total - one])
    tallies = jnp.asarray(profile(number_of, total, limit, skew), jnp.int32)
    twos = (number_of - 1) // 2
    giver, receiver = tallies[1:1 + 2 * twos:2], tallies[2:2 + 2 * twos:2]
    room = jnp.minimum(giver - 1, limit - receiver)
    passed = jax.random.randint(jax.random.fold_in(rng, 1), (twos,), 0, 1 << 20) % (room + 1)
    tallies = tallies.at[1:1 + 2 * twos:2].set(giver - passed).at[2:2 + 2 * twos:2].set(receiver + passed)
    return tallies[jax.random.permutation(jax.random.fold_in(rng, 2), number_of)]


def noise(rng, extent, width, reach, split=(), held_as=jnp.bfloat16):
    gain = levels(rng, extent, split, -0.22, 0.18) if split else 1.0
    entries = jax.random.normal(rng, extent, jnp.float32) * width * gain
    return jnp.minimum(jnp.maximum(entries, -reach), reach).astype(held_as)


def setup_inputs(seed: int = 0, part: int = 0) -> dict:
    arg_keys = jax.random.split(jax.random.key(seed), 6)
    part_splits = jax.random.split(jax.random.fold_in(arg_keys[5], part), 6)
    return {
        "acts": noise(part_splits[0], (LAYERS, TOKENS, D), 1.0, 6.0, ((0, 2), (1, 4), (2, 2))),
        "grads": noise(part_splits[1], (LAYERS, TOKENS, F), 1.0, 6.0, ((0, 2), (1, 4), (2, 2))),
        "query_left": noise(part_splits[2], (LAYERS, D, QR), D ** -0.5, 0.0625, ((0, 2), (1, 8))),
        "query_right": noise(part_splits[3], (LAYERS, F, QR), F ** -0.5, 0.03125, ((0, 2), (1, 8))),
        "seq_len": uneven(part_splits[4], SEQS, SEQS * LEN // 2, LEN, 2).astype(jnp.int32),
    }


def layer_scores(acts_layer, grads_layer, left_layer, right_layer, seq_len):
    proj_acts = jnp.dot(acts_layer, left_layer, preferred_element_type=jnp.float32)
    proj_grads = jnp.dot(grads_layer, right_layer, preferred_element_type=jnp.float32)
    product = (proj_acts * proj_grads).reshape(SEQS, LEN, QR)
    positions = jnp.arange(LEN, dtype=jnp.int32)
    live_mask = (positions[None, :] < seq_len[:, None]).astype(product.dtype)
    summed = lax.optimization_barrier(jnp.sum(product * live_mask[:, :, None], axis=1))
    return lax.optimization_barrier(jnp.sum(summed.reshape(SEQS, NQ, RANK), axis=2)) / math.sqrt(RANK * LEN)

def reference(acts, grads, query_left, query_right, seq_len):
    outputs = []
    for layer_index in range(LAYERS):
        outputs.append(layer_scores(acts[layer_index], grads[layer_index], query_left[layer_index], query_right[layer_index], seq_len))
    return jnp.stack(outputs)
```

```python
import functools
import math

import jax
import jax.numpy as jnp
from jax import lax
from jax.experimental import pallas as pl
from jax.experimental.pallas import tpu as pltpu
from jax.sharding import PartitionSpec as P

RANK = 8
LEN = 256
T = 256
LATE = 1
OFF = 11
MESH = pl.DeviceIdType.MESH


def seq_scores(proj_acts, proj_grads, live_mask):
    seq_count, seq_span = live_mask.shape
    product = (proj_acts * proj_grads).reshape(seq_count, seq_span, proj_acts.shape[1])
    summed = jnp.sum(product * live_mask[:, :, None], axis=1)
    return jnp.sum(summed.reshape(seq_count, -1, RANK), axis=2) / math.sqrt(RANK * LEN)


def on_device(acts, grads, query_left, query_right, seq_len):
    row_count = acts.shape[1]
    seq_count = seq_len.shape[0]
    seq_span = row_count // seq_count
    positions = lax.broadcasted_iota(jnp.int32, (seq_count, seq_span), 1)
    live_mask = (positions < seq_len[:, None]).astype(jnp.float32)
    proj_acts = jnp.dot(
        acts[0],
        lax.all_gather(query_left[0], "dp", axis=0, tiled=True),
        preferred_element_type=jnp.float32,
    )
    proj_grads = jnp.dot(
        grads[0],
        lax.all_gather(query_right[0], "dp", axis=0, tiled=True),
        preferred_element_type=jnp.float32,
    )
    share_acts = lax.psum_scatter(proj_acts, "mp", scatter_dimension=1, tiled=True)
    share_grads = lax.psum_scatter(proj_grads, "mp", scatter_dimension=1, tiled=True)
    share_scores = seq_scores(share_acts, share_grads, live_mask)
    return lax.all_gather(share_scores, "mp", axis=1, tiled=True)[None]


def line_kernel(
    left_rows, right_rows, acts, grads, ql, qr, seq_hbm, out,
    xa, wg, xb, acc, xacc, ra, live_a, got_a, psum, ret, sums, rsums, seq_len, cp,
    s_in, s_out, s_fwd_a, s_fwd_b, s_fwd_c, s_x, r_w, r_x, s_r, r_r,
):
    z = lax.axis_index("dp")
    m = lax.axis_index("mp")
    end = (z == 0) | (z == 3)
    inner = (z == 1) | (z == 2)
    step = jnp.where(z < 2, 1, -1)
    ahead = jnp.clip(z + step, 0, 3)
    behind = jnp.clip(z - step, 0, 3)
    far = jnp.clip(z + 2 * step, 0, 3)
    last = jnp.clip(z + 3 * step, 0, 3)
    peer = 1 - m

    a_cols = 4 * left_rows
    rows = left_rows + right_rows
    a_pieces, pieces = left_rows // T, rows // T
    keep = pieces - OFF
    half = acc.shape[1] // 2

    locals_ = [
        pltpu.make_async_copy(acts.at[0], xa.at[:, pl.ds(0, a_cols)], cp.at[0]),
        pltpu.make_async_copy(grads.at[0], xa.at[:, pl.ds(a_cols, 4 * right_rows)], cp.at[1]),
        pltpu.make_async_copy(ql.at[0], wg.at[pl.ds(pl.multiple_of(z * rows, T), left_rows)], cp.at[2]),
        pltpu.make_async_copy(
            qr.at[0], wg.at[pl.ds(pl.multiple_of(z * rows + left_rows, T), right_rows)], cp.at[3]
        ),
    ]

    lens = pltpu.make_async_copy(seq_hbm, seq_len, cp.at[4])

    barrier = pltpu.get_barrier_semaphore()
    pl.semaphore_signal(barrier, inc=1, device_id={"mp": peer}, device_id_type=MESH)
    pl.semaphore_signal(barrier, inc=1, device_id={"dp": ahead}, device_id_type=MESH)

    @pl.when(inner)
    def _():
        pl.semaphore_signal(barrier, inc=1, device_id={"dp": behind}, device_id_type=MESH)

    lens.start()
    for c in locals_:
        c.start()

    @pl.when(inner)
    def _():
        pl.semaphore_wait(barrier, 3)

    @pl.when(end)
    def _():
        pl.semaphore_wait(barrier, 2)

    def slot(owner, k):
        return wg.at[pl.ds(pl.multiple_of((owner * pieces + k) * T, T), T)]

    def piece_source(k):
        if k < a_pieces:
            return ql.at[0, pl.ds(k * T, T)]
        return qr.at[0, pl.ds((k - a_pieces) * T, T)]

    def send_own(k, to, sem):
        return pltpu.make_async_remote_copy(
            src_ref=piece_source(k), dst_ref=slot(z, k), send_sem=sem.at[k],
            recv_sem=r_w.at[z * pieces + k], device_id={"dp": to}, device_id_type=MESH,
        )

    def pass_on(owner, k, to, sem):
        return pltpu.make_async_remote_copy(
            src_ref=slot(owner, k), dst_ref=slot(owner, k), send_sem=sem.at[k],
            recv_sem=r_w.at[owner * pieces + k], device_id={"dp": to}, device_id_type=MESH,
        )

    def arrived(owner, k):
        pass_on(owner, k, ahead, s_fwd_a).wait_recv()

    def send_x(i):
        first = a_cols * 0 + ahead * right_rows + (keep - a_pieces + i) * T
        return pltpu.make_async_remote_copy(
            src_ref=grads.at[0, :, pl.ds(pl.multiple_of(first, T), T)], dst_ref=xb.at[i],
            send_sem=s_x.at[i], recv_sem=r_x.at[i], device_id={"dp": ahead}, device_id_type=MESH,
        )

    def multiply(owner, k):
        is_a = k < a_pieces
        col = jnp.where(
            is_a, owner * left_rows + k * T, a_cols + owner * right_rows + (k - a_pieces) * T
        )
        which = jnp.where(is_a, 0, 1)
        acc[which] += jnp.dot(
            xa[:, pl.ds(pl.multiple_of(col, T), T)], slot(owner, k)[...],
            preferred_element_type=jnp.float32,
        )

    def to_peer(src, dst, i):
        return pltpu.make_async_remote_copy(
            src_ref=src, dst_ref=dst, send_sem=s_r.at[i], recv_sem=r_r.at[i],
            device_id={"mp": peer}, device_id_type=MESH,
        )

    mine = pl.ds(pl.multiple_of(m * half, half), half)
    share_a = to_peer(acc.at[0], ra, 0)
    share_x = to_peer(got_a.at[mine], got_a.at[mine], 1)
    share_s = to_peer(sums, rsums, 2)

    def lend_a():
        return pltpu.make_async_remote_copy(
            src_ref=live_a.at[mine], dst_ref=got_a.at[mine], send_sem=s_r.at[3], recv_sem=r_r.at[3],
            device_id={"dp": ahead}, device_id_type=MESH,
        )

    def give_back():
        return pltpu.make_async_remote_copy(
            src_ref=psum, dst_ref=ret, send_sem=s_r.at[4], recv_sem=r_r.at[4],
            device_id={"dp": behind}, device_id_type=MESH,
        )

    def finish_a():
        share_a.wait_recv()
        row = lax.broadcasted_iota(jnp.int32, ra.shape, 0)
        stop = jnp.where(row < half, seq_len[0], half + seq_len[1])
        live_a[...] = jnp.where(row < stop, acc[0] + ra[...], 0.0)

    def row_sum(x):
        return jnp.broadcast_to(jnp.sum(x, axis=0, keepdims=True), sums.shape)

    def seq_sums(a_ref, g_ref):
        at = lax.broadcasted_iota(jnp.int32, sums.shape, 0)
        return jnp.where(
            at == 0,
            row_sum(a_ref[:half] * g_ref[:half]),
            row_sum(a_ref[half:] * g_ref[half:]),
        )

    @pl.when(end)
    def _():
        for k in range(pieces):
            send_own(k, ahead, s_in).start()
        for i in range(OFF - LATE):
            send_x(i).start()

    @pl.when(inner)
    def _():
        for k in range(pieces):
            send_own(k, ahead, s_in).start()
            if k < keep:
                send_own(k, behind, s_out).start()

    acc[...] = jnp.zeros_like(acc)
    lens.wait()
    for c in locals_:
        c.wait()

    @pl.when(end)
    def _():
        @pl.loop(0, pieces)
        def _(k):
            multiply(z, k)

        @pl.loop(0, keep)
        def _(k):
            arrived(ahead, k)
            multiply(ahead, k)

        @pl.loop(0, pieces)
        def _(k):
            arrived(far, k)
            multiply(far, k)

        @pl.loop(0, pieces)
        def _(k):
            arrived(last, k)
            multiply(last, k)

            @pl.when(k == a_pieces - 1)
            def _():
                share_a.start()

            @pl.when(k == a_pieces + 4)
            def _():
                finish_a()

            @pl.when(k == a_pieces + 5)
            def _():
                lend_a().start()
                for i in range(OFF - LATE, OFF):
                    send_x(i).start()

    @pl.when(inner)
    def _():
        xacc[...] = jnp.zeros_like(xacc)

        def take_x(i):
            pltpu.make_async_remote_copy(
                src_ref=xb.at[i], dst_ref=xb.at[i], send_sem=s_x.at[i], recv_sem=r_x.at[i],
                device_id={"dp": behind}, device_id_type=MESH,
            ).wait_recv()
            xacc[...] += jnp.dot(
                xb[i], slot(z, keep + i)[...], preferred_element_type=jnp.float32
            )

        @pl.loop(0, pieces)
        def _(k):
            arrived(ahead, k)
            pass_on(ahead, k, behind, s_fwd_a).start()
            arrived(behind, k)
            pass_on(behind, k, ahead, s_fwd_b).start()
            multiply(ahead, k)
            multiply(behind, k)
            multiply(z, k)

        @pl.loop(0, pieces)
        def _(k):
            arrived(far, k)
            pass_on(far, k, behind, s_fwd_c).start()
            multiply(far, k)

            @pl.when(k == a_pieces - 1)
            def _():
                share_a.start()

        finish_a()

        @pl.loop(0, OFF - LATE)
        def _(i):
            take_x(i)

        lend_a().wait_recv()
        share_x.start()
        share_x.wait_recv()

        @pl.loop(OFF - LATE, OFF)
        def _(i):
            take_x(i)

        psum[...] = seq_sums(got_a, xacc)
        give_back().start()

    sums[...] = seq_sums(live_a, acc.at[1])

    @pl.when(end)
    def _():
        give_back().wait_recv()
        sums[...] += ret[...]

    share_s.start()
    share_s.wait_recv()
    both = sums[...] + rsums[...]
    n_q = out.shape[2]
    qi = lax.broadcasted_iota(jnp.int32, (both.shape[1], n_q), 0)
    qj = lax.broadcasted_iota(jnp.int32, (both.shape[1], n_q), 1)
    pick = ((qi >= qj * RANK) & (qi < (qj + 1) * RANK)).astype(jnp.float32)
    scores = jnp.dot(
        both, pick, preferred_element_type=jnp.float32, precision=lax.Precision.HIGHEST
    )
    out[0] = scores[: out.shape[1]]

    share_a.wait_send()
    share_s.wait_send()

    @pl.when(end)
    def _():
        for i in range(OFF):
            send_x(i).wait_send()
        lend_a().wait_send()
        for k in range(pieces):
            send_own(k, ahead, s_in).wait_send()

    @pl.when(inner)
    def _():
        for k in range(pieces):
            send_own(k, ahead, s_in).wait_send()
            if k < keep:
                send_own(k, behind, s_out).wait_send()
            pass_on(ahead, k, behind, s_fwd_a).wait_send()
            pass_on(behind, k, ahead, s_fwd_b).wait_send()
            pass_on(far, k, behind, s_fwd_c).wait_send()
        share_x.wait_send()
        give_back().wait_send()


def on_line(acts, grads, query_left, query_right, seq_len):
    rows, cols = acts.shape[1], query_left.shape[2]
    left_rows, right_rows = query_left.shape[1], query_right.shape[1]
    pieces = (left_rows + right_rows) // T
    dma, f32, bf16 = pltpu.SemaphoreType.DMA, jnp.float32, jnp.bfloat16
    anywhere = pl.BlockSpec(memory_space=pltpu.HBM)
    return pl.pallas_call(
        functools.partial(line_kernel, left_rows, right_rows),
        out_shape=pltpu.VMEM((1, seq_len.shape[0], cols // RANK), f32),
        in_specs=[anywhere] * 5,
        out_specs=pl.BlockSpec(memory_space=pltpu.VMEM),
        scratch_shapes=[
            pltpu.VMEM((rows, acts.shape[2] + grads.shape[2]), bf16),
            pltpu.VMEM((4 * (left_rows + right_rows), cols), bf16),
            pltpu.VMEM((OFF, rows, T), bf16),
            pltpu.VMEM((2, rows, cols), f32),
            pltpu.VMEM((rows, cols), f32),
            pltpu.VMEM((rows, cols), f32),
            pltpu.VMEM((rows, cols), f32),
            pltpu.VMEM((rows, cols), f32),
            pltpu.VMEM((8, cols), f32),
            pltpu.VMEM((8, cols), f32),
            pltpu.VMEM((8, cols), f32),
            pltpu.VMEM((8, cols), f32),
            pltpu.SMEM((seq_len.shape[0],), jnp.int32),
            dma((5,)),
            dma((pieces,)),
            dma((pieces,)),
            dma((pieces,)),
            dma((pieces,)),
            dma((pieces,)),
            dma((OFF,)),
            dma((4 * pieces,)),
            dma((OFF,)),
            dma((5,)),
            dma((5,)),
        ],
        compiler_params=pltpu.CompilerParams(
            collective_id=0, has_side_effects=True, vmem_limit_bytes=60 * 1024 * 1024
        ),
    )(acts, grads, query_left, query_right, seq_len)


def fits_line(mesh, acts, query_left, query_right, seq_len):
    rows = acts.shape[1]
    pieces_g = query_right.shape[1] // T
    return (
        mesh.shape["dp"] == 4
        and mesh.shape["mp"] == 2
        and seq_len.shape[0] == 2
        and rows % 32 == 0
        and query_left.shape[1] % T == 0
        and query_right.shape[1] % T == 0
        and query_left.shape[1] >= T
        and pieces_g >= OFF
    )


def solution(mesh):
    def body(acts, grads, query_left, query_right, seq_len):
        if fits_line(mesh, acts, query_left, query_right, seq_len):
            summed = on_line(acts, grads, query_left, query_right, seq_len)
            return summed / math.sqrt(RANK * LEN)
        return on_device(acts, grads, query_left, query_right, seq_len)

    return jax.shard_map(
        body,
        mesh=mesh,
        in_specs=(
            P("layer", ("groups", "dp"), "mp"),
            P("layer", ("groups", "dp"), "mp"),
            P("layer", ("mp", "dp"), "groups"),
            P("layer", ("mp", "dp"), "groups"),
            P(("groups", "dp")),
        ),
        out_specs=P("layer", ("groups", "dp"), None),
        check_vma=False,
    )
```

```python
import functools
import math

import jax
import jax.numpy as jnp
from jax import lax
from jax.experimental import pallas as pl
from jax.experimental.pallas import tpu as pltpu
from jax.sharding import PartitionSpec as P

RANK = 8
LEN = 256
T = 256
LATE = 2
OFF = 11
MESH = pl.DeviceIdType.MESH


def seq_scores(proj_acts, proj_grads, live_mask):
    seq_count, seq_span = live_mask.shape
    product = (proj_acts * proj_grads).reshape(seq_count, seq_span, proj_acts.shape[1])
    summed = jnp.sum(product * live_mask[:, :, None], axis=1)
    return jnp.sum(summed.reshape(seq_count, -1, RANK), axis=2) / math.sqrt(RANK * LEN)


def on_device(acts, grads, query_left, query_right, seq_len):
    row_count = acts.shape[1]
    seq_count = seq_len.shape[0]
    seq_span = row_count // seq_count
    positions = lax.broadcasted_iota(jnp.int32, (seq_count, seq_span), 1)
    live_mask = (positions < seq_len[:, None]).astype(jnp.float32)
    proj_acts = jnp.dot(
        acts[0],
        lax.all_gather(query_left[0], "dp", axis=0, tiled=True),
        preferred_element_type=jnp.float32,
    )
    proj_grads = jnp.dot(
        grads[0],
        lax.all_gather(query_right[0], "dp", axis=0, tiled=True),
        preferred_element_type=jnp.float32,
    )
    share_acts = lax.psum_scatter(proj_acts, "mp", scatter_dimension=1, tiled=True)
    share_grads = lax.psum_scatter(proj_grads, "mp", scatter_dimension=1, tiled=True)
    share_scores = seq_scores(share_acts, share_grads, live_mask)
    return lax.all_gather(share_scores, "mp", axis=1, tiled=True)[None]


def line_kernel(
    left_rows, right_rows, acts, grads, ql, qr, seq_hbm, out,
    xa, wg, xb, acc, xacc, ra, live_a, got_a, psum, ret, sums, rsums, seq_len, cp,
    s_w, s_x, r_w, r_x, s_r, r_r,
):
    z = lax.axis_index("dp")
    m = lax.axis_index("mp")
    end = (z == 0) | (z == 3)
    inner = (z == 1) | (z == 2)
    step = jnp.where(z < 2, 1, -1)
    ahead = jnp.clip(z + step, 0, 3)
    behind = jnp.clip(z - step, 0, 3)
    far = jnp.clip(z + 2 * step, 0, 3)
    last = jnp.clip(z + 3 * step, 0, 3)
    peer = 1 - m

    a_cols = 4 * left_rows
    rows = left_rows + right_rows
    a_pieces, pieces = left_rows // T, rows // T
    keep, early = pieces - OFF, OFF - LATE
    half = acc.shape[1] // 2

    locals_ = [
        pltpu.make_async_copy(acts.at[0], xa.at[:, pl.ds(0, a_cols)], cp.at[0]),
        pltpu.make_async_copy(grads.at[0], xa.at[:, pl.ds(a_cols, 4 * right_rows)], cp.at[1]),
        pltpu.make_async_copy(ql.at[0], wg.at[pl.ds(pl.multiple_of(z * rows, T), left_rows)], cp.at[2]),
        pltpu.make_async_copy(
            qr.at[0], wg.at[pl.ds(pl.multiple_of(z * rows + left_rows, T), right_rows)], cp.at[3]
        ),
    ]

    lens = pltpu.make_async_copy(seq_hbm, seq_len, cp.at[4])

    barrier = pltpu.get_barrier_semaphore()
    pl.semaphore_signal(barrier, inc=1, device_id={"mp": peer}, device_id_type=MESH)
    pl.semaphore_signal(barrier, inc=1, device_id={"dp": ahead}, device_id_type=MESH)

    @pl.when(inner)
    def _():
        pl.semaphore_signal(barrier, inc=1, device_id={"dp": behind}, device_id_type=MESH)

    lens.start()
    for c in locals_:
        c.start()

    @pl.when(inner)
    def _():
        pl.semaphore_wait(barrier, 3)

    @pl.when(end)
    def _():
        pl.semaphore_wait(barrier, 2)

    def slot(owner, k):
        return wg.at[pl.ds(pl.multiple_of((owner * pieces + k) * T, T), T)]

    def landing(owner, k, at):
        return r_w.at[((owner - at + 3) % 4) * pieces + k]

    def piece_source(k):
        if k < a_pieces:
            return ql.at[0, pl.ds(k * T, T)]
        return qr.at[0, pl.ds((k - a_pieces) * T, T)]

    def send_own(k, to, sem):
        return pltpu.make_async_remote_copy(
            src_ref=piece_source(k), dst_ref=slot(z, k), send_sem=s_w.at[sem],
            recv_sem=landing(z, k, to), device_id={"dp": to}, device_id_type=MESH,
        )

    def pass_on(owner, k, to, sem):
        return pltpu.make_async_remote_copy(
            src_ref=slot(owner, k), dst_ref=slot(owner, k), send_sem=s_w.at[sem],
            recv_sem=landing(owner, k, to), device_id={"dp": to}, device_id_type=MESH,
        )

    def arrived(owner, k):
        pltpu.make_async_remote_copy(
            src_ref=slot(owner, k), dst_ref=slot(owner, k), send_sem=s_w.at[0],
            recv_sem=landing(owner, k, z), device_id={"dp": ahead}, device_id_type=MESH,
        ).wait_recv()

    def all_sent(sem, count, to):
        whole = wg.at[pl.ds(0, count * T)]
        pltpu.make_async_remote_copy(
            src_ref=whole, dst_ref=whole, send_sem=s_w.at[sem], recv_sem=r_w.at[0],
            device_id={"dp": to}, device_id_type=MESH,
        ).wait_send()

    def send_x(i):
        skip, count = (0, early) if i == 0 else (early + i - 1, 1)
        first = ahead * right_rows + (keep - a_pieces + skip) * T
        return pltpu.make_async_remote_copy(
            src_ref=grads.at[0, :, pl.ds(pl.multiple_of(first, T), count * T)],
            dst_ref=xb.at[:, pl.ds(skip * T, count * T)], send_sem=s_x.at[i], recv_sem=r_x.at[i],
            device_id={"dp": ahead}, device_id_type=MESH,
        )

    def multiply(owner, k):
        is_a = k < a_pieces
        col = jnp.where(
            is_a, owner * left_rows + k * T, a_cols + owner * right_rows + (k - a_pieces) * T
        )
        which = jnp.where(is_a, 0, 1)
        acc[which] += jnp.dot(
            xa[:, pl.ds(pl.multiple_of(col, T), T)], slot(owner, k)[...],
            preferred_element_type=jnp.float32,
        )

    def to_peer(src, dst, i):
        return pltpu.make_async_remote_copy(
            src_ref=src, dst_ref=dst, send_sem=s_r.at[i], recv_sem=r_r.at[i],
            device_id={"mp": peer}, device_id_type=MESH,
        )

    mine = pl.ds(pl.multiple_of(m * half, half), half)
    share_a = to_peer(acc.at[0], ra, 0)
    share_x = to_peer(got_a.at[mine], got_a.at[mine], 1)
    share_s = to_peer(sums, rsums, 2)

    def lend_a():
        return pltpu.make_async_remote_copy(
            src_ref=live_a.at[mine], dst_ref=got_a.at[mine], send_sem=s_r.at[3], recv_sem=r_r.at[3],
            device_id={"dp": ahead}, device_id_type=MESH,
        )

    def give_back():
        return pltpu.make_async_remote_copy(
            src_ref=psum, dst_ref=ret, send_sem=s_r.at[4], recv_sem=r_r.at[4],
            device_id={"dp": behind}, device_id_type=MESH,
        )

    def finish_a():
        share_a.wait_recv()
        row = lax.broadcasted_iota(jnp.int32, ra.shape, 0)
        stop = jnp.where(row < half, seq_len[0], half + seq_len[1])
        live_a[...] = jnp.where(row < stop, acc[0] + ra[...], 0.0)

    def row_sum(x):
        return jnp.broadcast_to(jnp.sum(x, axis=0, keepdims=True), sums.shape)

    def seq_sums(a_ref, g_ref):
        at = lax.broadcasted_iota(jnp.int32, sums.shape, 0)
        return jnp.where(
            at == 0,
            row_sum(a_ref[:half] * g_ref[:half]),
            row_sum(a_ref[half:] * g_ref[half:]),
        )

    @pl.when(end)
    def _():
        for k in range(pieces):
            send_own(k, ahead, 0).start()
        send_x(0).start()

    @pl.when(inner)
    def _():
        for k in range(pieces):
            send_own(k, ahead, 0).start()
            if k < keep:
                send_own(k, behind, 1).start()

    acc[...] = jnp.zeros_like(acc)
    lens.wait()
    for c in locals_:
        c.wait()

    @pl.when(end)
    def _():
        @pl.loop(0, pieces)
        def _(k):
            multiply(z, k)

        @pl.loop(0, keep)
        def _(k):
            arrived(ahead, k)
            multiply(ahead, k)

        @pl.loop(0, pieces)
        def _(k):
            arrived(far, k)
            multiply(far, k)

        @pl.loop(0, pieces)
        def _(k):
            arrived(last, k)
            multiply(last, k)

            @pl.when(k == a_pieces - 1)
            def _():
                share_a.start()

            @pl.when(k == a_pieces + 4)
            def _():
                finish_a()

            @pl.when(k == a_pieces + 5)
            def _():
                lend_a().start()
                for i in range(1, LATE + 1):
                    send_x(i).start()

    @pl.when(inner)
    def _():
        xacc[...] = jnp.zeros_like(xacc)

        def x_here(i):
            skip, count = (0, early) if i == 0 else (early + i - 1, 1)
            part = xb.at[:, pl.ds(skip * T, count * T)]
            pltpu.make_async_remote_copy(
                src_ref=part, dst_ref=part, send_sem=s_x.at[i], recv_sem=r_x.at[i],
                device_id={"dp": behind}, device_id_type=MESH,
            ).wait_recv()

        def take_x(i):
            xacc[...] += jnp.dot(
                xb[:, pl.ds(pl.multiple_of(i * T, T), T)], slot(z, keep + i)[...],
                preferred_element_type=jnp.float32,
            )

        @pl.loop(0, pieces)
        def _(k):
            arrived(ahead, k)
            pass_on(ahead, k, behind, 2).start()
            arrived(behind, k)
            pass_on(behind, k, ahead, 3).start()
            multiply(ahead, k)
            multiply(behind, k)
            multiply(z, k)

        @pl.loop(0, pieces)
        def _(k):
            arrived(far, k)
            pass_on(far, k, behind, 4).start()
            multiply(far, k)

            @pl.when(k == a_pieces - 1)
            def _():
                share_a.start()

        finish_a()

        x_here(0)

        @pl.loop(0, early)
        def _(i):
            take_x(i)

        lend_a().wait_recv()
        share_x.start()
        share_x.wait_recv()

        for i in range(1, LATE + 1):
            x_here(i)
            take_x(early + i - 1)

        psum[...] = seq_sums(got_a, xacc)
        give_back().start()

    sums[...] = seq_sums(live_a, acc.at[1])

    @pl.when(end)
    def _():
        give_back().wait_recv()
        sums[...] += ret[...]

    share_s.start()
    share_s.wait_recv()
    both = sums[...] + rsums[...]
    n_q = out.shape[2]
    qi = lax.broadcasted_iota(jnp.int32, (both.shape[1], n_q), 0)
    qj = lax.broadcasted_iota(jnp.int32, (both.shape[1], n_q), 1)
    pick = ((qi >= qj * RANK) & (qi < (qj + 1) * RANK)).astype(jnp.float32)
    scores = jnp.dot(
        both, pick, preferred_element_type=jnp.float32, precision=lax.Precision.HIGHEST
    )
    out[0] = scores[: out.shape[1]]

    share_a.wait_send()
    share_s.wait_send()

    @pl.when(end)
    def _():
        for i in range(LATE + 1):
            send_x(i).wait_send()
        lend_a().wait_send()
        all_sent(0, pieces, ahead)

    @pl.when(inner)
    def _():
        all_sent(0, pieces, ahead)
        all_sent(1, keep, behind)
        all_sent(2, pieces, behind)
        all_sent(3, pieces, ahead)
        all_sent(4, pieces, behind)
        share_x.wait_send()
        give_back().wait_send()


def on_line(acts, grads, query_left, query_right, seq_len):
    rows, cols = acts.shape[1], query_left.shape[2]
    left_rows, right_rows = query_left.shape[1], query_right.shape[1]
    pieces = (left_rows + right_rows) // T
    dma, f32, bf16 = pltpu.SemaphoreType.DMA, jnp.float32, jnp.bfloat16
    anywhere = pl.BlockSpec(memory_space=pltpu.HBM)
    return pl.pallas_call(
        functools.partial(line_kernel, left_rows, right_rows),
        out_shape=pltpu.VMEM((1, seq_len.shape[0], cols // RANK), f32),
        in_specs=[anywhere] * 5,
        out_specs=pl.BlockSpec(memory_space=pltpu.VMEM),
        scratch_shapes=[
            pltpu.VMEM((rows, acts.shape[2] + grads.shape[2]), bf16),
            pltpu.VMEM((4 * (left_rows + right_rows), cols), bf16),
            pltpu.VMEM((rows, OFF * T), bf16),
            pltpu.VMEM((2, rows, cols), f32),
            pltpu.VMEM((rows, cols), f32),
            pltpu.VMEM((rows, cols), f32),
            pltpu.VMEM((rows, cols), f32),
            pltpu.VMEM((rows, cols), f32),
            pltpu.VMEM((8, cols), f32),
            pltpu.VMEM((8, cols), f32),
            pltpu.VMEM((8, cols), f32),
            pltpu.VMEM((8, cols), f32),
            pltpu.SMEM((seq_len.shape[0],), jnp.int32),
            dma((5,)),
            dma((5,)),
            dma((LATE + 1,)),
            dma((3 * pieces,)),
            dma((LATE + 1,)),
            dma((5,)),
            dma((5,)),
        ],
        compiler_params=pltpu.CompilerParams(
            collective_id=0, has_side_effects=True, vmem_limit_bytes=60 * 1024 * 1024
        ),
    )(acts, grads, query_left, query_right, seq_len)


def fits_line(mesh, acts, query_left, query_right, seq_len):
    rows = acts.shape[1]
    pieces_g = query_right.shape[1] // T
    return (
        mesh.shape["dp"] == 4
        and mesh.shape["mp"] == 2
        and seq_len.shape[0] == 2
        and rows % 32 == 0
        and query_left.shape[1] % T == 0
        and query_right.shape[1] % T == 0
        and query_left.shape[1] >= T
        and pieces_g >= OFF
    )


def solution(mesh):
    def body(acts, grads, query_left, query_right, seq_len):
        if fits_line(mesh, acts, query_left, query_right, seq_len):
            summed = on_line(acts, grads, query_left, query_right, seq_len)
            return summed / math.sqrt(RANK * LEN)
        return on_device(acts, grads, query_left, query_right, seq_len)

    return jax.shard_map(
        body,
        mesh=mesh,
        in_specs=(
            P("layer", ("groups", "dp"), "mp"),
            P("layer", ("groups", "dp"), "mp"),
            P("layer", ("mp", "dp"), "groups"),
            P("layer", ("mp", "dp"), "groups"),
            P(("groups", "dp")),
        ),
        out_specs=P("layer", ("groups", "dp"), None),
        check_vma=False,
    )
```

```python
import functools
import math

import jax
import jax.numpy as jnp
from jax import lax
from jax.experimental import pallas as pl
from jax.experimental.pallas import tpu as pltpu
from jax.sharding import PartitionSpec as P

RANK = 8
LEN = 256
T = 256
LATE = 2
OFF = 11
MESH = pl.DeviceIdType.MESH


def seq_scores(proj_acts, proj_grads, live_mask):
    seq_count, seq_span = live_mask.shape
    product = (proj_acts * proj_grads).reshape(seq_count, seq_span, proj_acts.shape[1])
    summed = jnp.sum(product * live_mask[:, :, None], axis=1)
    return jnp.sum(summed.reshape(seq_count, -1, RANK), axis=2) / math.sqrt(RANK * LEN)


def on_device(acts, grads, query_left, query_right, seq_len):
    row_count = acts.shape[1]
    seq_count = seq_len.shape[0]
    seq_span = row_count // seq_count
    positions = lax.broadcasted_iota(jnp.int32, (seq_count, seq_span), 1)
    live_mask = (positions < seq_len[:, None]).astype(jnp.float32)
    proj_acts = jnp.dot(
        acts[0],
        lax.all_gather(query_left[0], "dp", axis=0, tiled=True),
        preferred_element_type=jnp.float32,
    )
    proj_grads = jnp.dot(
        grads[0],
        lax.all_gather(query_right[0], "dp", axis=0, tiled=True),
        preferred_element_type=jnp.float32,
    )
    share_acts = lax.psum_scatter(proj_acts, "mp", scatter_dimension=1, tiled=True)
    share_grads = lax.psum_scatter(proj_grads, "mp", scatter_dimension=1, tiled=True)
    share_scores = seq_scores(share_acts, share_grads, live_mask)
    return lax.all_gather(share_scores, "mp", axis=1, tiled=True)[None]


def line_kernel(
    left_rows, right_rows, acts, grads, ql, qr, seq_hbm, out,
    xa, wg, xb, acc, xacc, ra, live_a, got_a, psum, ret, sums, rsums, seq_len, cp,
    s_w, s_x, r_w, r_x, s_r, r_r,
):
    z = lax.axis_index("dp")
    yields = lax.axis_index("layer") == 1
    m = lax.axis_index("mp")
    end = (z == 0) | (z == 3)
    inner = (z == 1) | (z == 2)
    step = jnp.where(z < 2, 1, -1)
    ahead = jnp.clip(z + step, 0, 3)
    behind = jnp.clip(z - step, 0, 3)
    far = jnp.clip(z + 2 * step, 0, 3)
    last = jnp.clip(z + 3 * step, 0, 3)
    peer = 1 - m

    a_cols = 4 * left_rows
    rows = left_rows + right_rows
    a_pieces, pieces = left_rows // T, rows // T
    keep, early = pieces - OFF, OFF - LATE
    half = acc.shape[1] // 2

    acts_in = pltpu.make_async_copy(acts.at[0], xa.at[:, pl.ds(0, a_cols)], cp.at[0])
    others_in = [
        pltpu.make_async_copy(grads.at[0], xa.at[:, pl.ds(a_cols, 4 * right_rows)], cp.at[1]),
        pltpu.make_async_copy(ql.at[0], wg.at[pl.ds(pl.multiple_of(z * rows, T), left_rows)], cp.at[2]),
        pltpu.make_async_copy(
            qr.at[0], wg.at[pl.ds(pl.multiple_of(z * rows + left_rows, T), right_rows)], cp.at[3]
        ),
    ]
    lens = pltpu.make_async_copy(seq_hbm, seq_len, cp.at[4])

    barrier = pltpu.get_barrier_semaphore()
    pl.semaphore_signal(barrier, inc=1, device_id={"mp": peer}, device_id_type=MESH)
    pl.semaphore_signal(barrier, inc=1, device_id={"dp": ahead}, device_id_type=MESH)

    @pl.when(inner)
    def _():
        pl.semaphore_signal(barrier, inc=1, device_id={"dp": behind}, device_id_type=MESH)

    lens.start()
    acts_in.start()
    for c in others_in:
        c.start()

    @pl.when(inner)
    def _():
        pl.semaphore_wait(barrier, 3)

    @pl.when(end)
    def _():
        pl.semaphore_wait(barrier, 2)

    def slot(owner, k):
        return wg.at[pl.ds(pl.multiple_of((owner * pieces + k) * T, T), T)]

    def landing(owner, k, at):
        return r_w.at[((owner - at + 3) % 4) * pieces + k]

    def piece_source(k):
        if k < a_pieces:
            return ql.at[0, pl.ds(k * T, T)]
        return qr.at[0, pl.ds((k - a_pieces) * T, T)]

    def send_own(k, to, sem):
        return pltpu.make_async_remote_copy(
            src_ref=piece_source(k), dst_ref=slot(z, k), send_sem=s_w.at[sem],
            recv_sem=landing(z, k, to), device_id={"dp": to}, device_id_type=MESH,
        )

    def pass_on(owner, k, to, sem):
        return pltpu.make_async_remote_copy(
            src_ref=slot(owner, k), dst_ref=slot(owner, k), send_sem=s_w.at[sem],
            recv_sem=landing(owner, k, to), device_id={"dp": to}, device_id_type=MESH,
        )

    def arrived(owner, k):
        pltpu.make_async_remote_copy(
            src_ref=slot(owner, k), dst_ref=slot(owner, k), send_sem=s_w.at[0],
            recv_sem=landing(owner, k, z), device_id={"dp": ahead}, device_id_type=MESH,
        ).wait_recv()

    def all_sent(sem, count, to):
        whole = wg.at[pl.ds(0, count * T)]
        pltpu.make_async_remote_copy(
            src_ref=whole, dst_ref=whole, send_sem=s_w.at[sem], recv_sem=r_w.at[0],
            device_id={"dp": to}, device_id_type=MESH,
        ).wait_send()

    def send_x(i):
        skip, count = (0, early) if i == 0 else (early + i - 1, 1)
        first = ahead * right_rows + (keep - a_pieces + skip) * T
        return pltpu.make_async_remote_copy(
            src_ref=grads.at[0, :, pl.ds(pl.multiple_of(first, T), count * T)],
            dst_ref=xb.at[:, pl.ds(skip * T, count * T)], send_sem=s_x.at[i], recv_sem=r_x.at[i],
            device_id={"dp": ahead}, device_id_type=MESH,
        )

    def multiply(owner, k):
        is_a = k < a_pieces
        col = jnp.where(
            is_a, owner * left_rows + k * T, a_cols + owner * right_rows + (k - a_pieces) * T
        )
        which = jnp.where(is_a, 0, 1)
        acc[which] += jnp.dot(
            xa[:, pl.ds(pl.multiple_of(col, T), T)], slot(owner, k)[...],
            preferred_element_type=jnp.float32,
        )

    def to_peer(src, dst, i):
        return pltpu.make_async_remote_copy(
            src_ref=src, dst_ref=dst, send_sem=s_r.at[i], recv_sem=r_r.at[i],
            device_id={"mp": peer}, device_id_type=MESH,
        )

    mine = pl.ds(pl.multiple_of(m * half, half), half)
    share_a = to_peer(acc.at[0], ra, 0)
    share_x = to_peer(got_a.at[mine], got_a.at[mine], 1)
    share_s = to_peer(sums, rsums, 2)

    def lend_a():
        return pltpu.make_async_remote_copy(
            src_ref=live_a.at[mine], dst_ref=got_a.at[mine], send_sem=s_r.at[3], recv_sem=r_r.at[3],
            device_id={"dp": ahead}, device_id_type=MESH,
        )

    def give_back():
        return pltpu.make_async_remote_copy(
            src_ref=psum, dst_ref=ret, send_sem=s_r.at[4], recv_sem=r_r.at[4],
            device_id={"dp": behind}, device_id_type=MESH,
        )

    def finish_a():
        share_a.wait_recv()
        row = lax.broadcasted_iota(jnp.int32, ra.shape, 0)
        stop = jnp.where(row < half, seq_len[0], half + seq_len[1])
        live_a[...] = jnp.where(row < stop, acc[0] + ra[...], 0.0)

    def row_sum(x):
        return jnp.broadcast_to(jnp.sum(x, axis=0, keepdims=True), sums.shape)

    def seq_sums(a_ref, g_ref):
        at = lax.broadcasted_iota(jnp.int32, sums.shape, 0)
        return jnp.where(
            at == 0,
            row_sum(a_ref[:half] * g_ref[:half]),
            row_sum(a_ref[half:] * g_ref[half:]),
        )

    @pl.when(yields)
    def _():
        acts_in.wait()

    @pl.when(end)
    def _():
        for k in range(pieces):
            send_own(k, ahead, 0).start()
        send_x(0).start()

    @pl.when(inner)
    def _():
        for k in range(pieces):
            send_own(k, ahead, 0).start()
            if k < keep:
                send_own(k, behind, 1).start()

    acc[...] = jnp.zeros_like(acc)
    lens.wait()
    for c in others_in:
        c.wait()

    @pl.when(jnp.logical_not(yields))
    def _():
        acts_in.wait()

    @pl.when(end)
    def _():
        @pl.loop(0, pieces)
        def _(k):
            multiply(z, k)

        @pl.loop(0, keep)
        def _(k):
            arrived(ahead, k)
            multiply(ahead, k)

        @pl.loop(0, pieces)
        def _(k):
            arrived(far, k)
            multiply(far, k)

        @pl.loop(0, pieces)
        def _(k):
            arrived(last, k)
            multiply(last, k)

            @pl.when(k == a_pieces - 1)
            def _():
                share_a.start()

            @pl.when(k == a_pieces + 4)
            def _():
                finish_a()

            @pl.when(k == a_pieces + 5)
            def _():
                lend_a().start()
                for i in range(1, LATE + 1):
                    send_x(i).start()

    @pl.when(inner)
    def _():
        xacc[...] = jnp.zeros_like(xacc)

        def x_here(i):
            skip, count = (0, early) if i == 0 else (early + i - 1, 1)
            part = xb.at[:, pl.ds(skip * T, count * T)]
            pltpu.make_async_remote_copy(
                src_ref=part, dst_ref=part, send_sem=s_x.at[i], recv_sem=r_x.at[i],
                device_id={"dp": behind}, device_id_type=MESH,
            ).wait_recv()

        def take_x(i):
            xacc[...] += jnp.dot(
                xb[:, pl.ds(pl.multiple_of(i * T, T), T)], slot(z, keep + i)[...],
                preferred_element_type=jnp.float32,
            )

        @pl.loop(0, pieces)
        def _(k):
            arrived(ahead, k)
            pass_on(ahead, k, behind, 2).start()
            arrived(behind, k)
            pass_on(behind, k, ahead, 3).start()
            multiply(ahead, k)
            multiply(behind, k)
            multiply(z, k)

        @pl.loop(0, pieces)
        def _(k):
            arrived(far, k)
            pass_on(far, k, behind, 4).start()
            multiply(far, k)

            @pl.when(k == a_pieces - 1)
            def _():
                share_a.start()

        finish_a()

        x_here(0)

        @pl.loop(0, early)
        def _(i):
            take_x(i)

        lend_a().wait_recv()
        share_x.start()
        share_x.wait_recv()

        for i in range(1, LATE + 1):
            x_here(i)
            take_x(early + i - 1)

        psum[...] = seq_sums(got_a, xacc)
        give_back().start()

    sums[...] = seq_sums(live_a, acc.at[1])

    @pl.when(end)
    def _():
        give_back().wait_recv()
        sums[...] += ret[...]

    share_s.start()
    share_s.wait_recv()
    both = sums[...] + rsums[...]
    n_q = out.shape[2]
    qi = lax.broadcasted_iota(jnp.int32, (both.shape[1], n_q), 0)
    qj = lax.broadcasted_iota(jnp.int32, (both.shape[1], n_q), 1)
    pick = ((qi >= qj * RANK) & (qi < (qj + 1) * RANK)).astype(jnp.float32)
    scores = jnp.dot(
        both, pick, preferred_element_type=jnp.float32, precision=lax.Precision.HIGHEST
    )
    out[0] = scores[: out.shape[1]]

    share_a.wait_send()
    share_s.wait_send()

    @pl.when(end)
    def _():
        for i in range(LATE + 1):
            send_x(i).wait_send()
        lend_a().wait_send()
        all_sent(0, pieces, ahead)

    @pl.when(inner)
    def _():
        all_sent(0, pieces, ahead)
        all_sent(1, keep, behind)
        all_sent(2, pieces, behind)
        all_sent(3, pieces, ahead)
        all_sent(4, pieces, behind)
        share_x.wait_send()
        give_back().wait_send()


def on_line(acts, grads, query_left, query_right, seq_len):
    rows, cols = acts.shape[1], query_left.shape[2]
    left_rows, right_rows = query_left.shape[1], query_right.shape[1]
    pieces = (left_rows + right_rows) // T
    dma, f32, bf16 = pltpu.SemaphoreType.DMA, jnp.float32, jnp.bfloat16
    anywhere = pl.BlockSpec(memory_space=pltpu.HBM)
    return pl.pallas_call(
        functools.partial(line_kernel, left_rows, right_rows),
        out_shape=pltpu.VMEM((1, seq_len.shape[0], cols // RANK), f32),
        in_specs=[anywhere] * 5,
        out_specs=pl.BlockSpec(memory_space=pltpu.VMEM),
        scratch_shapes=[
            pltpu.VMEM((rows, acts.shape[2] + grads.shape[2]), bf16),
            pltpu.VMEM((4 * (left_rows + right_rows), cols), bf16),
            pltpu.VMEM((rows, OFF * T), bf16),
            pltpu.VMEM((2, rows, cols), f32),
            pltpu.VMEM((rows, cols), f32),
            pltpu.VMEM((rows, cols), f32),
            pltpu.VMEM((rows, cols), f32),
            pltpu.VMEM((rows, cols), f32),
            pltpu.VMEM((8, cols), f32),
            pltpu.VMEM((8, cols), f32),
            pltpu.VMEM((8, cols), f32),
            pltpu.VMEM((8, cols), f32),
            pltpu.SMEM((seq_len.shape[0],), jnp.int32),
            dma((5,)),
            dma((5,)),
            dma((LATE + 1,)),
            dma((3 * pieces,)),
            dma((LATE + 1,)),
            dma((5,)),
            dma((5,)),
        ],
        compiler_params=pltpu.CompilerParams(
            collective_id=0, has_side_effects=True, vmem_limit_bytes=60 * 1024 * 1024
        ),
    )(acts, grads, query_left, query_right, seq_len)


def fits_line(mesh, acts, query_left, query_right, seq_len):
    rows = acts.shape[1]
    pieces_g = query_right.shape[1] // T
    return (
        mesh.shape["dp"] == 4
        and mesh.shape["mp"] == 2
        and seq_len.shape[0] == 2
        and rows % 32 == 0
        and query_left.shape[1] % T == 0
        and query_right.shape[1] % T == 0
        and query_left.shape[1] >= T
        and pieces_g >= OFF
    )


def solution(mesh):
    def body(acts, grads, query_left, query_right, seq_len):
        if fits_line(mesh, acts, query_left, query_right, seq_len):
            summed = on_line(acts, grads, query_left, query_right, seq_len)
            return summed / math.sqrt(RANK * LEN)
        return on_device(acts, grads, query_left, query_right, seq_len)

    return jax.shard_map(
        body,
        mesh=mesh,
        in_specs=(
            P("layer", ("groups", "dp"), "mp"),
            P("layer", ("groups", "dp"), "mp"),
            P("layer", ("mp", "dp"), "groups"),
            P("layer", ("mp", "dp"), "groups"),
            P(("groups", "dp")),
        ),
        out_specs=P("layer", ("groups", "dp"), None),
        check_vma=False,
    )
```

```python
import functools
import math

import jax
import jax.numpy as jnp
from jax import lax
from jax.experimental import pallas as pl
from jax.experimental.pallas import tpu as pltpu
from jax.sharding import PartitionSpec as P

RANK = 8
LEN = 256
T = 256
LATE = 2
OFF = 11
MESH = pl.DeviceIdType.MESH


def seq_scores(proj_acts, proj_grads, live_mask):
    seq_count, seq_span = live_mask.shape
    product = (proj_acts * proj_grads).reshape(seq_count, seq_span, proj_acts.shape[1])
    summed = jnp.sum(product * live_mask[:, :, None], axis=1)
    return jnp.sum(summed.reshape(seq_count, -1, RANK), axis=2) / math.sqrt(RANK * LEN)


def on_device(acts, grads, query_left, query_right, seq_len):
    row_count = acts.shape[1]
    seq_count = seq_len.shape[0]
    seq_span = row_count // seq_count
    positions = lax.broadcasted_iota(jnp.int32, (seq_count, seq_span), 1)
    live_mask = (positions < seq_len[:, None]).astype(jnp.float32)
    proj_acts = jnp.dot(
        acts[0],
        lax.all_gather(query_left[0], "dp", axis=0, tiled=True),
        preferred_element_type=jnp.float32,
    )
    proj_grads = jnp.dot(
        grads[0],
        lax.all_gather(query_right[0], "dp", axis=0, tiled=True),
        preferred_element_type=jnp.float32,
    )
    share_acts = lax.psum_scatter(proj_acts, "mp", scatter_dimension=1, tiled=True)
    share_grads = lax.psum_scatter(proj_grads, "mp", scatter_dimension=1, tiled=True)
    share_scores = seq_scores(share_acts, share_grads, live_mask)
    return lax.all_gather(share_scores, "mp", axis=1, tiled=True)[None]


def line_kernel(
    left_rows, right_rows, acts, grads, ql, qr, seq_hbm, out,
    xa, wg, xb, acc, xacc, ra, live_a, got_a, psum, ret, sums, rsums, seq_len, cp,
    s_w, s_x, r_w, r_x, s_r, r_r,
):
    z = lax.axis_index("dp")
    m = lax.axis_index("mp")
    end = (z == 0) | (z == 3)
    inner = (z == 1) | (z == 2)
    step = jnp.where(z < 2, 1, -1)
    ahead = jnp.clip(z + step, 0, 3)
    behind = jnp.clip(z - step, 0, 3)
    far = jnp.clip(z + 2 * step, 0, 3)
    last = jnp.clip(z + 3 * step, 0, 3)
    peer = 1 - m

    a_cols = 4 * left_rows
    rows = left_rows + right_rows
    a_pieces, pieces = left_rows // T, rows // T
    keep, early = pieces - OFF, OFF - LATE
    half = acc.shape[1] // 2

    rows_in = [
        pltpu.make_async_copy(acts.at[0], xa.at[:, pl.ds(0, a_cols)], cp.at[0]),
        pltpu.make_async_copy(grads.at[0], xa.at[:, pl.ds(a_cols, 4 * right_rows)], cp.at[1]),
    ]
    own_in = [
        pltpu.make_async_copy(ql.at[0], wg.at[pl.ds(pl.multiple_of(z * rows, T), left_rows)], cp.at[2]),
        pltpu.make_async_copy(
            qr.at[0], wg.at[pl.ds(pl.multiple_of(z * rows + left_rows, T), right_rows)], cp.at[3]
        ),
    ]
    lens = pltpu.make_async_copy(seq_hbm, seq_len, cp.at[4])

    barrier = pltpu.get_barrier_semaphore()
    pl.semaphore_signal(barrier, inc=1, device_id={"mp": peer}, device_id_type=MESH)
    pl.semaphore_signal(barrier, inc=1, device_id={"dp": ahead}, device_id_type=MESH)

    @pl.when(inner)
    def _():
        pl.semaphore_signal(barrier, inc=1, device_id={"dp": behind}, device_id_type=MESH)

    lens.start()
    for c in own_in:
        c.start()

    @pl.when(inner)
    def _():
        pl.semaphore_wait(barrier, 3)

    @pl.when(end)
    def _():
        pl.semaphore_wait(barrier, 2)

    def slot(owner, k):
        return wg.at[pl.ds(pl.multiple_of((owner * pieces + k) * T, T), T)]

    def landing(owner, k, at):
        return r_w.at[((owner - at + 3) % 4) * pieces + k]

    def send_own(k, to, sem):
        return pltpu.make_async_remote_copy(
            src_ref=slot(z, k), dst_ref=slot(z, k), send_sem=s_w.at[sem],
            recv_sem=landing(z, k, to), device_id={"dp": to}, device_id_type=MESH,
        )

    def pass_on(owner, k, to, sem):
        return pltpu.make_async_remote_copy(
            src_ref=slot(owner, k), dst_ref=slot(owner, k), send_sem=s_w.at[sem],
            recv_sem=landing(owner, k, to), device_id={"dp": to}, device_id_type=MESH,
        )

    def arrived(owner, k):
        pltpu.make_async_remote_copy(
            src_ref=slot(owner, k), dst_ref=slot(owner, k), send_sem=s_w.at[0],
            recv_sem=landing(owner, k, z), device_id={"dp": ahead}, device_id_type=MESH,
        ).wait_recv()

    def all_sent(sem, count, to):
        whole = wg.at[pl.ds(0, count * T)]
        pltpu.make_async_remote_copy(
            src_ref=whole, dst_ref=whole, send_sem=s_w.at[sem], recv_sem=r_w.at[0],
            device_id={"dp": to}, device_id_type=MESH,
        ).wait_send()

    def send_x(i):
        skip, count = (0, early) if i == 0 else (early + i - 1, 1)
        first = ahead * right_rows + (keep - a_pieces + skip) * T
        return pltpu.make_async_remote_copy(
            src_ref=grads.at[0, :, pl.ds(pl.multiple_of(first, T), count * T)],
            dst_ref=xb.at[:, pl.ds(skip * T, count * T)], send_sem=s_x.at[i], recv_sem=r_x.at[i],
            device_id={"dp": ahead}, device_id_type=MESH,
        )

    def multiply(owner, k):
        is_a = k < a_pieces
        col = jnp.where(
            is_a, owner * left_rows + k * T, a_cols + owner * right_rows + (k - a_pieces) * T
        )
        which = jnp.where(is_a, 0, 1)
        acc[which] += jnp.dot(
            xa[:, pl.ds(pl.multiple_of(col, T), T)], slot(owner, k)[...],
            preferred_element_type=jnp.float32,
        )

    def to_peer(src, dst, i):
        return pltpu.make_async_remote_copy(
            src_ref=src, dst_ref=dst, send_sem=s_r.at[i], recv_sem=r_r.at[i],
            device_id={"mp": peer}, device_id_type=MESH,
        )

    mine = pl.ds(pl.multiple_of(m * half, half), half)
    share_a = to_peer(acc.at[0], ra, 0)
    share_x = to_peer(got_a.at[mine], got_a.at[mine], 1)
    share_s = to_peer(sums, rsums, 2)

    def lend_a():
        return pltpu.make_async_remote_copy(
            src_ref=live_a.at[mine], dst_ref=got_a.at[mine], send_sem=s_r.at[3], recv_sem=r_r.at[3],
            device_id={"dp": ahead}, device_id_type=MESH,
        )

    def give_back():
        return pltpu.make_async_remote_copy(
            src_ref=psum, dst_ref=ret, send_sem=s_r.at[4], recv_sem=r_r.at[4],
            device_id={"dp": behind}, device_id_type=MESH,
        )

    def finish_a():
        share_a.wait_recv()
        row = lax.broadcasted_iota(jnp.int32, ra.shape, 0)
        stop = jnp.where(row < half, seq_len[0], half + seq_len[1])
        live_a[...] = jnp.where(row < stop, acc[0] + ra[...], 0.0)

    def row_sum(x):
        return jnp.broadcast_to(jnp.sum(x, axis=0, keepdims=True), sums.shape)

    def seq_sums(a_ref, g_ref):
        at = lax.broadcasted_iota(jnp.int32, sums.shape, 0)
        return jnp.where(
            at == 0,
            row_sum(a_ref[:half] * g_ref[:half]),
            row_sum(a_ref[half:] * g_ref[half:]),
        )

    for c in own_in:
        c.wait()

    @pl.when(end)
    def _():
        for k in range(pieces):
            send_own(k, ahead, 0).start()
        send_x(0).start()

    @pl.when(inner)
    def _():
        for k in range(pieces):
            send_own(k, ahead, 0).start()
            if k < keep:
                send_own(k, behind, 1).start()

    for c in rows_in:
        c.start()
    acc[...] = jnp.zeros_like(acc)
    lens.wait()
    for c in rows_in:
        c.wait()

    @pl.when(end)
    def _():
        @pl.loop(0, pieces)
        def _(k):
            multiply(z, k)

        @pl.loop(0, keep)
        def _(k):
            arrived(ahead, k)
            multiply(ahead, k)

        @pl.loop(0, pieces)
        def _(k):
            arrived(far, k)
            multiply(far, k)

        @pl.loop(0, pieces)
        def _(k):
            arrived(last, k)
            multiply(last, k)

            @pl.when(k == a_pieces - 1)
            def _():
                share_a.start()

            @pl.when(k == a_pieces + 4)
            def _():
                finish_a()

            @pl.when(k == a_pieces + 5)
            def _():
                lend_a().start()
                for i in range(1, LATE + 1):
                    send_x(i).start()

    @pl.when(inner)
    def _():
        xacc[...] = jnp.zeros_like(xacc)

        def x_here(i):
            skip, count = (0, early) if i == 0 else (early + i - 1, 1)
            part = xb.at[:, pl.ds(skip * T, count * T)]
            pltpu.make_async_remote_copy(
                src_ref=part, dst_ref=part, send_sem=s_x.at[i], recv_sem=r_x.at[i],
                device_id={"dp": behind}, device_id_type=MESH,
            ).wait_recv()

        def take_x(i):
            xacc[...] += jnp.dot(
                xb[:, pl.ds(pl.multiple_of(i * T, T), T)], slot(z, keep + i)[...],
                preferred_element_type=jnp.float32,
            )

        @pl.loop(0, pieces)
        def _(k):
            arrived(ahead, k)
            pass_on(ahead, k, behind, 2).start()
            arrived(behind, k)
            pass_on(behind, k, ahead, 3).start()
            multiply(ahead, k)
            multiply(behind, k)
            multiply(z, k)

        @pl.loop(0, pieces)
        def _(k):
            arrived(far, k)
            pass_on(far, k, behind, 4).start()
            multiply(far, k)

            @pl.when(k == a_pieces - 1)
            def _():
                share_a.start()

        finish_a()

        x_here(0)

        @pl.loop(0, early)
        def _(i):
            take_x(i)

        lend_a().wait_recv()
        share_x.start()
        share_x.wait_recv()

        for i in range(1, LATE + 1):
            x_here(i)
            take_x(early + i - 1)

        psum[...] = seq_sums(got_a, xacc)
        give_back().start()

    sums[...] = seq_sums(live_a, acc.at[1])

    @pl.when(end)
    def _():
        give_back().wait_recv()
        sums[...] += ret[...]

    share_s.start()
    share_s.wait_recv()
    both = sums[...] + rsums[...]
    n_q = out.shape[2]
    qi = lax.broadcasted_iota(jnp.int32, (both.shape[1], n_q), 0)
    qj = lax.broadcasted_iota(jnp.int32, (both.shape[1], n_q), 1)
    pick = ((qi >= qj * RANK) & (qi < (qj + 1) * RANK)).astype(jnp.float32)
    scores = jnp.dot(
        both, pick, preferred_element_type=jnp.float32, precision=lax.Precision.HIGHEST
    )
    out[0] = scores[: out.shape[1]]

    share_a.wait_send()
    share_s.wait_send()

    @pl.when(end)
    def _():
        for i in range(LATE + 1):
            send_x(i).wait_send()
        lend_a().wait_send()
        all_sent(0, pieces, ahead)

    @pl.when(inner)
    def _():
        all_sent(0, pieces, ahead)
        all_sent(1, keep, behind)
        all_sent(2, pieces, behind)
        all_sent(3, pieces, ahead)
        all_sent(4, pieces, behind)
        share_x.wait_send()
        give_back().wait_send()


def on_line(acts, grads, query_left, query_right, seq_len):
    rows, cols = acts.shape[1], query_left.shape[2]
    left_rows, right_rows = query_left.shape[1], query_right.shape[1]
    pieces = (left_rows + right_rows) // T
    dma, f32, bf16 = pltpu.SemaphoreType.DMA, jnp.float32, jnp.bfloat16
    anywhere = pl.BlockSpec(memory_space=pltpu.HBM)
    return pl.pallas_call(
        functools.partial(line_kernel, left_rows, right_rows),
        out_shape=pltpu.VMEM((1, seq_len.shape[0], cols // RANK), f32),
        in_specs=[anywhere] * 5,
        out_specs=pl.BlockSpec(memory_space=pltpu.VMEM),
        scratch_shapes=[
            pltpu.VMEM((rows, acts.shape[2] + grads.shape[2]), bf16),
            pltpu.VMEM((4 * (left_rows + right_rows), cols), bf16),
            pltpu.VMEM((rows, OFF * T), bf16),
            pltpu.VMEM((2, rows, cols), f32),
            pltpu.VMEM((rows, cols), f32),
            pltpu.VMEM((rows, cols), f32),
            pltpu.VMEM((rows, cols), f32),
            pltpu.VMEM((rows, cols), f32),
            pltpu.VMEM((8, cols), f32),
            pltpu.VMEM((8, cols), f32),
            pltpu.VMEM((8, cols), f32),
            pltpu.VMEM((8, cols), f32),
            pltpu.SMEM((seq_len.shape[0],), jnp.int32),
            dma((5,)),
            dma((5,)),
            dma((LATE + 1,)),
            dma((3 * pieces,)),
            dma((LATE + 1,)),
            dma((5,)),
            dma((5,)),
        ],
        compiler_params=pltpu.CompilerParams(
            collective_id=0, has_side_effects=True, vmem_limit_bytes=60 * 1024 * 1024
        ),
    )(acts, grads, query_left, query_right, seq_len)


def fits_line(mesh, acts, query_left, query_right, seq_len):
    rows = acts.shape[1]
    pieces_g = query_right.shape[1] // T
    return (
        mesh.shape["dp"] == 4
        and mesh.shape["mp"] == 2
        and seq_len.shape[0] == 2
        and rows % 32 == 0
        and query_left.shape[1] % T == 0
        and query_right.shape[1] % T == 0
        and query_left.shape[1] >= T
        and pieces_g >= OFF
    )


def solution(mesh):
    def body(acts, grads, query_left, query_right, seq_len):
        if fits_line(mesh, acts, query_left, query_right, seq_len):
            summed = on_line(acts, grads, query_left, query_right, seq_len)
            return summed / math.sqrt(RANK * LEN)
        return on_device(acts, grads, query_left, query_right, seq_len)

    return jax.shard_map(
        body,
        mesh=mesh,
        in_specs=(
            P("layer", ("groups", "dp"), "mp"),
            P("layer", ("groups", "dp"), "mp"),
            P("layer", ("mp", "dp"), "groups"),
            P("layer", ("mp", "dp"), "groups"),
            P(("groups", "dp")),
        ),
        out_specs=P("layer", ("groups", "dp"), None),
        check_vma=False,
    )
```

```python
import functools
import math

import jax
import jax.numpy as jnp
from jax import lax
from jax.experimental import pallas as pl
from jax.experimental.pallas import tpu as pltpu
from jax.sharding import PartitionSpec as P

RANK = 8
LEN = 256
T = 256
LATE = 2
OFF = 11
MESH = pl.DeviceIdType.MESH


def seq_scores(proj_acts, proj_grads, live_mask):
    seq_count, seq_span = live_mask.shape
    product = (proj_acts * proj_grads).reshape(seq_count, seq_span, proj_acts.shape[1])
    summed = jnp.sum(product * live_mask[:, :, None], axis=1)
    return jnp.sum(summed.reshape(seq_count, -1, RANK), axis=2) / math.sqrt(RANK * LEN)


def on_device(acts, grads, query_left, query_right, seq_len):
    row_count = acts.shape[1]
    seq_count = seq_len.shape[0]
    seq_span = row_count // seq_count
    positions = lax.broadcasted_iota(jnp.int32, (seq_count, seq_span), 1)
    live_mask = (positions < seq_len[:, None]).astype(jnp.float32)
    proj_acts = jnp.dot(
        acts[0],
        lax.all_gather(query_left[0], "dp", axis=0, tiled=True),
        preferred_element_type=jnp.float32,
    )
    proj_grads = jnp.dot(
        grads[0],
        lax.all_gather(query_right[0], "dp", axis=0, tiled=True),
        preferred_element_type=jnp.float32,
    )
    share_acts = lax.psum_scatter(proj_acts, "mp", scatter_dimension=1, tiled=True)
    share_grads = lax.psum_scatter(proj_grads, "mp", scatter_dimension=1, tiled=True)
    share_scores = seq_scores(share_acts, share_grads, live_mask)
    return lax.all_gather(share_scores, "mp", axis=1, tiled=True)[None]


def line_kernel(
    left_rows, right_rows, acts, grads, ql, qr, seq_hbm, out,
    xa, wg, xb, acc, xacc, ra, live_a, got_a, psum, ret, sums, rsums, seq_len, cp,
    s_w, s_x, r_w, r_x, s_r, r_r,
):
    z = lax.axis_index("dp")
    m = lax.axis_index("mp")
    end = (z == 0) | (z == 3)
    inner = (z == 1) | (z == 2)
    step = jnp.where(z < 2, 1, -1)
    ahead = jnp.clip(z + step, 0, 3)
    behind = jnp.clip(z - step, 0, 3)
    far = jnp.clip(z + 2 * step, 0, 3)
    last = jnp.clip(z + 3 * step, 0, 3)
    peer = 1 - m

    a_cols = 4 * left_rows
    rows = left_rows + right_rows
    a_pieces, pieces = left_rows // T, rows // T
    keep, early = pieces - OFF, OFF - LATE
    half = acc.shape[1] // 2

    locals_ = [
        pltpu.make_async_copy(acts.at[0], xa.at[:, pl.ds(0, a_cols)], cp.at[0]),
        pltpu.make_async_copy(grads.at[0], xa.at[:, pl.ds(a_cols, 4 * right_rows)], cp.at[1]),
        pltpu.make_async_copy(ql.at[0], wg.at[pl.ds(pl.multiple_of(z * rows, T), left_rows)], cp.at[2]),
        pltpu.make_async_copy(
            qr.at[0], wg.at[pl.ds(pl.multiple_of(z * rows + left_rows, T), right_rows)], cp.at[3]
        ),
    ]

    lens = pltpu.make_async_copy(seq_hbm, seq_len, cp.at[4])

    barrier = pltpu.get_barrier_semaphore()
    pl.semaphore_signal(barrier, inc=1, device_id={"mp": peer}, device_id_type=MESH)
    pl.semaphore_signal(barrier, inc=1, device_id={"dp": ahead}, device_id_type=MESH)

    @pl.when(inner)
    def _():
        pl.semaphore_signal(barrier, inc=1, device_id={"dp": behind}, device_id_type=MESH)

    lens.start()
    for c in locals_:
        c.start()

    @pl.when(inner)
    def _():
        pl.semaphore_wait(barrier, 3)

    @pl.when(end)
    def _():
        pl.semaphore_wait(barrier, 2)

    def slot(owner, k):
        return wg.at[pl.ds(pl.multiple_of((owner * pieces + k) * T, T), T)]

    def landing(owner, k, at):
        return r_w.at[((owner - at + 3) % 4) * pieces + k]

    def piece_source(k):
        if k < a_pieces:
            return ql.at[0, pl.ds(k * T, T)]
        return qr.at[0, pl.ds((k - a_pieces) * T, T)]

    def send_own(k, to, sem):
        return pltpu.make_async_remote_copy(
            src_ref=piece_source(k), dst_ref=slot(z, k), send_sem=s_w.at[sem],
            recv_sem=landing(z, k, to), device_id={"dp": to}, device_id_type=MESH,
        )

    def pass_on(owner, k, to, sem):
        return pltpu.make_async_remote_copy(
            src_ref=slot(owner, k), dst_ref=slot(owner, k), send_sem=s_w.at[sem],
            recv_sem=landing(owner, k, to), device_id={"dp": to}, device_id_type=MESH,
        )

    def arrived(owner, k):
        pltpu.make_async_remote_copy(
            src_ref=slot(owner, k), dst_ref=slot(owner, k), send_sem=s_w.at[0],
            recv_sem=landing(owner, k, z), device_id={"dp": ahead}, device_id_type=MESH,
        ).wait_recv()

    def all_sent(sem, count, to):
        whole = wg.at[pl.ds(0, count * T)]
        pltpu.make_async_remote_copy(
            src_ref=whole, dst_ref=whole, send_sem=s_w.at[sem], recv_sem=r_w.at[0],
            device_id={"dp": to}, device_id_type=MESH,
        ).wait_send()

    def send_x(i):
        skip, count = (0, early) if i == 0 else (early + i - 1, 1)
        first = ahead * right_rows + (keep - a_pieces + skip) * T
        return pltpu.make_async_remote_copy(
            src_ref=grads.at[0, :, pl.ds(pl.multiple_of(first, T), count * T)],
            dst_ref=xb.at[:, pl.ds(skip * T, count * T)], send_sem=s_x.at[i], recv_sem=r_x.at[i],
            device_id={"dp": ahead}, device_id_type=MESH,
        )

    def multiply(owner, k):
        is_a = k < a_pieces
        col = jnp.where(
            is_a, owner * left_rows + k * T, a_cols + owner * right_rows + (k - a_pieces) * T
        )
        which = jnp.where(is_a, 0, 1)
        acc[which] += jnp.dot(
            xa[:, pl.ds(pl.multiple_of(col, T), T)], slot(owner, k)[...],
            preferred_element_type=jnp.float32,
        )

    def to_peer(src, dst, i):
        return pltpu.make_async_remote_copy(
            src_ref=src, dst_ref=dst, send_sem=s_r.at[i], recv_sem=r_r.at[i],
            device_id={"mp": peer}, device_id_type=MESH,
        )

    mine = pl.ds(pl.multiple_of(m * half, half), half)
    share_a = to_peer(acc.at[0], ra, 0)
    share_x = to_peer(got_a.at[mine], got_a.at[mine], 1)
    share_s = to_peer(sums, rsums, 2)

    def lend_a():
        return pltpu.make_async_remote_copy(
            src_ref=live_a.at[mine], dst_ref=got_a.at[mine], send_sem=s_r.at[3], recv_sem=r_r.at[3],
            device_id={"dp": ahead}, device_id_type=MESH,
        )

    def give_back():
        return pltpu.make_async_remote_copy(
            src_ref=psum, dst_ref=ret, send_sem=s_r.at[4], recv_sem=r_r.at[4],
            device_id={"dp": behind}, device_id_type=MESH,
        )

    def finish_a():
        share_a.wait_recv()
        row = lax.broadcasted_iota(jnp.int32, ra.shape, 0)
        stop = jnp.where(row < half, seq_len[0], half + seq_len[1])
        live_a[...] = jnp.where(row < stop, acc[0] + ra[...], 0.0)

    def row_sum(x):
        return jnp.broadcast_to(jnp.sum(x, axis=0, keepdims=True), sums.shape)

    def seq_sums(a_ref, g_ref):
        at = lax.broadcasted_iota(jnp.int32, sums.shape, 0)
        return jnp.where(
            at == 0,
            row_sum(a_ref[:half] * g_ref[:half]),
            row_sum(a_ref[half:] * g_ref[half:]),
        )

    @pl.when(end)
    def _():
        for k in range(pieces):
            send_own(k, ahead, 0).start()
        send_x(0).start()

    @pl.when(inner)
    def _():
        for k in range(pieces):
            send_own(k, ahead, 0).start()
            if k < keep:
                send_own(k, behind, 1).start()

    acc[...] = jnp.zeros_like(acc)
    lens.wait()
    for c in locals_:
        c.wait()

    @pl.when(end)
    def _():
        @pl.loop(0, pieces)
        def _(k):
            multiply(z, k)

        @pl.loop(0, keep)
        def _(k):
            arrived(ahead, k)
            multiply(ahead, k)

        @pl.loop(0, pieces)
        def _(k):
            arrived(far, k)
            multiply(far, k)

        @pl.loop(0, pieces)
        def _(k):
            arrived(last, k)
            multiply(last, k)

            @pl.when(k == a_pieces - 1)
            def _():
                share_a.start()

            @pl.when(k == a_pieces + 4)
            def _():
                finish_a()

            @pl.when(k == a_pieces + 5)
            def _():
                lend_a().start()
                for i in range(1, LATE + 1):
                    send_x(i).start()

    @pl.when(inner)
    def _():
        xacc[...] = jnp.zeros_like(xacc)

        def x_here(i):
            skip, count = (0, early) if i == 0 else (early + i - 1, 1)
            part = xb.at[:, pl.ds(skip * T, count * T)]
            pltpu.make_async_remote_copy(
                src_ref=part, dst_ref=part, send_sem=s_x.at[i], recv_sem=r_x.at[i],
                device_id={"dp": behind}, device_id_type=MESH,
            ).wait_recv()

        def take_x(i):
            xacc[...] += jnp.dot(
                xb[:, pl.ds(pl.multiple_of(i * T, T), T)], slot(z, keep + i)[...],
                preferred_element_type=jnp.float32,
            )

        @pl.loop(0, pieces)
        def _(k):
            arrived(ahead, k)
            pass_on(ahead, k, behind, 2).start()
            arrived(behind, k)
            pass_on(behind, k, ahead, 3).start()
            multiply(ahead, k)
            multiply(behind, k)
            multiply(z, k)

        @pl.loop(0, pieces)
        def _(k):
            arrived(far, k)
            pass_on(far, k, behind, 4).start()
            multiply(far, k)

            @pl.when(k == a_pieces - 1)
            def _():
                share_a.start()

        finish_a()

        x_here(0)

        @pl.loop(0, early)
        def _(i):
            take_x(i)

        lend_a().wait_recv()
        share_x.start()
        share_x.wait_recv()

        for i in range(1, LATE + 1):
            x_here(i)
            take_x(early + i - 1)

        psum[...] = seq_sums(got_a, xacc)
        give_back().start()

    sums[...] = seq_sums(live_a, acc.at[1])

    @pl.when(end)
    def _():
        give_back().wait_recv()
        sums[...] += ret[...]

    share_s.start()

    @pl.when(end)
    def _():
        for i in range(LATE + 1):
            send_x(i).wait_send()
        lend_a().wait_send()
        all_sent(0, pieces, ahead)

    share_s.wait_recv()
    both = sums[...] + rsums[...]
    n_q = out.shape[2]
    qi = lax.broadcasted_iota(jnp.int32, (both.shape[1], n_q), 0)
    qj = lax.broadcasted_iota(jnp.int32, (both.shape[1], n_q), 1)
    pick = ((qi >= qj * RANK) & (qi < (qj + 1) * RANK)).astype(jnp.float32)
    scores = jnp.dot(
        both, pick, preferred_element_type=jnp.float32, precision=lax.Precision.HIGHEST
    )
    out[0] = scores[: out.shape[1]] / math.sqrt(RANK * LEN)

    share_a.wait_send()
    share_s.wait_send()

    @pl.when(inner)
    def _():
        all_sent(0, pieces, ahead)
        all_sent(1, keep, behind)
        all_sent(2, pieces, behind)
        all_sent(3, pieces, ahead)
        all_sent(4, pieces, behind)
        share_x.wait_send()
        give_back().wait_send()


def on_line(acts, grads, query_left, query_right, seq_len):
    rows, cols = acts.shape[1], query_left.shape[2]
    left_rows, right_rows = query_left.shape[1], query_right.shape[1]
    pieces = (left_rows + right_rows) // T
    dma, f32, bf16 = pltpu.SemaphoreType.DMA, jnp.float32, jnp.bfloat16
    anywhere = pl.BlockSpec(memory_space=pltpu.HBM)
    return pl.pallas_call(
        functools.partial(line_kernel, left_rows, right_rows),
        out_shape=pltpu.VMEM((1, seq_len.shape[0], cols // RANK), f32),
        in_specs=[anywhere] * 5,
        out_specs=pl.BlockSpec(memory_space=pltpu.VMEM),
        scratch_shapes=[
            pltpu.VMEM((rows, acts.shape[2] + grads.shape[2]), bf16),
            pltpu.VMEM((4 * (left_rows + right_rows), cols), bf16),
            pltpu.VMEM((rows, OFF * T), bf16),
            pltpu.VMEM((2, rows, cols), f32),
            pltpu.VMEM((rows, cols), f32),
            pltpu.VMEM((rows, cols), f32),
            pltpu.VMEM((rows, cols), f32),
            pltpu.VMEM((rows, cols), f32),
            pltpu.VMEM((8, cols), f32),
            pltpu.VMEM((8, cols), f32),
            pltpu.VMEM((8, cols), f32),
            pltpu.VMEM((8, cols), f32),
            pltpu.SMEM((seq_len.shape[0],), jnp.int32),
            dma((5,)),
            dma((5,)),
            dma((LATE + 1,)),
            dma((3 * pieces,)),
            dma((LATE + 1,)),
            dma((5,)),
            dma((5,)),
        ],
        compiler_params=pltpu.CompilerParams(
            collective_id=0, has_side_effects=True, vmem_limit_bytes=60 * 1024 * 1024
        ),
    )(acts, grads, query_left, query_right, seq_len)


def fits_line(mesh, acts, query_left, query_right, seq_len):
    rows = acts.shape[1]
    pieces_g = query_right.shape[1] // T
    return (
        mesh.shape["dp"] == 4
        and mesh.shape["mp"] == 2
        and seq_len.shape[0] == 2
        and rows % 32 == 0
        and query_left.shape[1] % T == 0
        and query_right.shape[1] % T == 0
        and query_left.shape[1] >= T
        and pieces_g >= OFF
    )


def solution(mesh):
    def body(acts, grads, query_left, query_right, seq_len):
        if fits_line(mesh, acts, query_left, query_right, seq_len):
            return on_line(acts, grads, query_left, query_right, seq_len)
        return on_device(acts, grads, query_left, query_right, seq_len)

    return jax.shard_map(
        body,
        mesh=mesh,
        in_specs=(
            P("layer", ("groups", "dp"), "mp"),
            P("layer", ("groups", "dp"), "mp"),
            P("layer", ("mp", "dp"), "groups"),
            P("layer", ("mp", "dp"), "groups"),
            P(("groups", "dp")),
        ),
        out_specs=P("layer", ("groups", "dp"), None),
        check_vma=False,
    )
```

```python
import functools
import math

import jax
import jax.numpy as jnp
from jax import lax
from jax.experimental import pallas as pl
from jax.experimental.pallas import tpu as pltpu
from jax.sharding import PartitionSpec as P

RANK = 8
LEN = 256
T = 256
LATE = 2
OFF = 11
MESH = pl.DeviceIdType.MESH


def seq_scores(proj_acts, proj_grads, live_mask):
    seq_count, seq_span = live_mask.shape
    product = (proj_acts * proj_grads).reshape(seq_count, seq_span, proj_acts.shape[1])
    summed = jnp.sum(product * live_mask[:, :, None], axis=1)
    return jnp.sum(summed.reshape(seq_count, -1, RANK), axis=2) / math.sqrt(RANK * LEN)


def on_device(acts, grads, query_left, query_right, seq_len):
    row_count = acts.shape[1]
    seq_count = seq_len.shape[0]
    seq_span = row_count // seq_count
    positions = lax.broadcasted_iota(jnp.int32, (seq_count, seq_span), 1)
    live_mask = (positions < seq_len[:, None]).astype(jnp.float32)
    proj_acts = jnp.dot(
        acts[0],
        lax.all_gather(query_left[0], "dp", axis=0, tiled=True),
        preferred_element_type=jnp.float32,
    )
    proj_grads = jnp.dot(
        grads[0],
        lax.all_gather(query_right[0], "dp", axis=0, tiled=True),
        preferred_element_type=jnp.float32,
    )
    share_acts = lax.psum_scatter(proj_acts, "mp", scatter_dimension=1, tiled=True)
    share_grads = lax.psum_scatter(proj_grads, "mp", scatter_dimension=1, tiled=True)
    share_scores = seq_scores(share_acts, share_grads, live_mask)
    return lax.all_gather(share_scores, "mp", axis=1, tiled=True)[None]


def line_kernel(
    left_rows, right_rows, acts, grads, ql, qr, seq_hbm, out,
    xa, wg, xb, acc, xacc, ra, live_a, got_a, psum, ret, sums, rsums, seq_len, cp,
    s_w, s_x, r_w, r_x, s_r, r_r,
):
    z = lax.axis_index("dp")
    m = lax.axis_index("mp")
    end = (z == 0) | (z == 3)
    inner = (z == 1) | (z == 2)
    step = jnp.where(z < 2, 1, -1)
    ahead = jnp.clip(z + step, 0, 3)
    behind = jnp.clip(z - step, 0, 3)
    far = jnp.clip(z + 2 * step, 0, 3)
    last = jnp.clip(z + 3 * step, 0, 3)
    peer = 1 - m

    a_cols = 4 * left_rows
    rows = left_rows + right_rows
    a_pieces, pieces = left_rows // T, rows // T
    keep, early = pieces - OFF, OFF - LATE
    half = acc.shape[1] // 2

    locals_ = [
        pltpu.make_async_copy(acts.at[0], xa.at[:, pl.ds(0, a_cols)], cp.at[0]),
        pltpu.make_async_copy(grads.at[0], xa.at[:, pl.ds(a_cols, 4 * right_rows)], cp.at[1]),
        pltpu.make_async_copy(ql.at[0], wg.at[pl.ds(pl.multiple_of(z * rows, T), left_rows)], cp.at[2]),
        pltpu.make_async_copy(
            qr.at[0], wg.at[pl.ds(pl.multiple_of(z * rows + left_rows, T), right_rows)], cp.at[3]
        ),
    ]

    lens = pltpu.make_async_copy(seq_hbm, seq_len, cp.at[4])

    barrier = pltpu.get_barrier_semaphore()
    pl.semaphore_signal(barrier, inc=1, device_id={"mp": peer}, device_id_type=MESH)
    pl.semaphore_signal(barrier, inc=1, device_id={"dp": ahead}, device_id_type=MESH)

    @pl.when(inner)
    def _():
        pl.semaphore_signal(barrier, inc=1, device_id={"dp": behind}, device_id_type=MESH)

    lens.start()
    for c in locals_:
        c.start()

    @pl.when(inner)
    def _():
        pl.semaphore_wait(barrier, 3)

    @pl.when(end)
    def _():
        pl.semaphore_wait(barrier, 2)

    def slot(owner, k):
        return wg.at[pl.ds(pl.multiple_of((owner * pieces + k) * T, T), T)]

    def landing(owner, k, at):
        return r_w.at[((owner - at + 3) % 4) * pieces + k]

    def piece_source(k):
        if k < a_pieces:
            return ql.at[0, pl.ds(k * T, T)]
        return qr.at[0, pl.ds((k - a_pieces) * T, T)]

    def send_own(k, to, sem):
        return pltpu.make_async_remote_copy(
            src_ref=piece_source(k), dst_ref=slot(z, k), send_sem=s_w.at[sem],
            recv_sem=landing(z, k, to), device_id={"dp": to}, device_id_type=MESH,
        )

    def pass_on(owner, k, to, sem):
        return pltpu.make_async_remote_copy(
            src_ref=slot(owner, k), dst_ref=slot(owner, k), send_sem=s_w.at[sem],
            recv_sem=landing(owner, k, to), device_id={"dp": to}, device_id_type=MESH,
        )

    def arrived(owner, k):
        pltpu.make_async_remote_copy(
            src_ref=slot(owner, k), dst_ref=slot(owner, k), send_sem=s_w.at[0],
            recv_sem=landing(owner, k, z), device_id={"dp": ahead}, device_id_type=MESH,
        ).wait_recv()

    def all_sent(sem, count, to):
        whole = wg.at[pl.ds(0, count * T)]
        pltpu.make_async_remote_copy(
            src_ref=whole, dst_ref=whole, send_sem=s_w.at[sem], recv_sem=r_w.at[0],
            device_id={"dp": to}, device_id_type=MESH,
        ).wait_send()

    def send_x(i):
        skip, count = (0, early) if i == 0 else (early + i - 1, 1)
        first = ahead * right_rows + (keep - a_pieces + skip) * T
        return pltpu.make_async_remote_copy(
            src_ref=grads.at[0, :, pl.ds(pl.multiple_of(first, T), count * T)],
            dst_ref=xb.at[:, pl.ds(skip * T, count * T)], send_sem=s_x.at[i], recv_sem=r_x.at[i],
            device_id={"dp": ahead}, device_id_type=MESH,
        )

    def multiply(owner, k):
        is_a = k < a_pieces
        col = jnp.where(
            is_a, owner * left_rows + k * T, a_cols + owner * right_rows + (k - a_pieces) * T
        )
        which = jnp.where(is_a, 0, 1)
        acc[which] += jnp.dot(
            xa[:, pl.ds(pl.multiple_of(col, T), T)], slot(owner, k)[...],
            preferred_element_type=jnp.float32,
        )

    def to_peer(src, dst, i):
        return pltpu.make_async_remote_copy(
            src_ref=src, dst_ref=dst, send_sem=s_r.at[i], recv_sem=r_r.at[i],
            device_id={"mp": peer}, device_id_type=MESH,
        )

    mine = pl.ds(pl.multiple_of(m * half, half), half)
    share_a = to_peer(acc.at[0], ra, 0)
    share_x = to_peer(got_a.at[mine], got_a.at[mine], 1)
    share_s = to_peer(sums, rsums, 2)

    def lend_a():
        return pltpu.make_async_remote_copy(
            src_ref=live_a.at[mine], dst_ref=got_a.at[mine], send_sem=s_r.at[3], recv_sem=r_r.at[3],
            device_id={"dp": ahead}, device_id_type=MESH,
        )

    def give_back():
        return pltpu.make_async_remote_copy(
            src_ref=psum, dst_ref=ret, send_sem=s_r.at[4], recv_sem=r_r.at[4],
            device_id={"dp": behind}, device_id_type=MESH,
        )

    def finish_a():
        share_a.wait_recv()
        row = lax.broadcasted_iota(jnp.int32, ra.shape, 0)
        stop = jnp.where(row < half, seq_len[0], half + seq_len[1])
        live_a[...] = jnp.where(row < stop, acc[0] + ra[...], 0.0)

    def row_sum(x):
        return jnp.broadcast_to(jnp.sum(x, axis=0, keepdims=True), sums.shape)

    def seq_sums(a_ref, g_ref):
        at = lax.broadcasted_iota(jnp.int32, sums.shape, 0)
        return jnp.where(
            at == 0,
            row_sum(a_ref[:half] * g_ref[:half]),
            row_sum(a_ref[half:] * g_ref[half:]),
        )

    @pl.when(end)
    def _():
        for k in range(pieces):
            send_own(k, ahead, 0).start()
        send_x(0).start()

    @pl.when(inner)
    def _():
        for k in range(pieces):
            send_own(k, ahead, 0).start()
            if k < keep:
                send_own(k, behind, 1).start()

    acc[...] = jnp.zeros_like(acc)
    lens.wait()
    for c in locals_:
        c.wait()

    @pl.when(end)
    def _():
        @pl.loop(0, pieces)
        def _(k):
            multiply(z, k)

        @pl.loop(0, keep)
        def _(k):
            arrived(ahead, k)
            multiply(ahead, k)

        @pl.loop(0, pieces)
        def _(k):
            arrived(far, k)
            multiply(far, k)

        @pl.loop(0, pieces)
        def _(k):
            arrived(last, k)
            multiply(last, k)

            @pl.when(k == a_pieces - 1)
            def _():
                share_a.start()

            @pl.when(k == a_pieces + 4)
            def _():
                finish_a()

            @pl.when(k == a_pieces + 5)
            def _():
                lend_a().start()
                for i in range(1, LATE + 1):
                    send_x(i).start()

    @pl.when(inner)
    def _():
        xacc[...] = jnp.zeros_like(xacc)

        def x_here(i):
            skip, count = (0, early) if i == 0 else (early + i - 1, 1)
            part = xb.at[:, pl.ds(skip * T, count * T)]
            pltpu.make_async_remote_copy(
                src_ref=part, dst_ref=part, send_sem=s_x.at[i], recv_sem=r_x.at[i],
                device_id={"dp": behind}, device_id_type=MESH,
            ).wait_recv()

        def take_x(i):
            xacc[...] += jnp.dot(
                xb[:, pl.ds(pl.multiple_of(i * T, T), T)], slot(z, keep + i)[...],
                preferred_element_type=jnp.float32,
            )

        @pl.loop(0, pieces)
        def _(k):
            arrived(ahead, k)
            pass_on(ahead, k, behind, 2).start()
            arrived(behind, k)
            pass_on(behind, k, ahead, 3).start()
            multiply(ahead, k)
            multiply(behind, k)
            multiply(z, k)

        @pl.loop(0, pieces)
        def _(k):
            arrived(far, k)
            pass_on(far, k, behind, 4).start()
            multiply(far, k)

            @pl.when(k == a_pieces - 1)
            def _():
                share_a.start()

        finish_a()

        x_here(0)

        @pl.loop(0, early)
        def _(i):
            take_x(i)

        lend_a().wait_recv()
        share_x.start()
        share_x.wait_recv()

        for i in range(1, LATE + 1):
            x_here(i)
            take_x(early + i - 1)

        psum[...] = seq_sums(got_a, xacc)
        give_back().start()

    sums[...] = seq_sums(live_a, acc.at[1])

    @pl.when(end)
    def _():
        give_back().wait_recv()
        sums[...] += ret[...]

    share_s.start()

    @pl.when(end)
    def _():
        for i in range(LATE + 1):
            send_x(i).wait_send()
        lend_a().wait_send()
        all_sent(0, pieces, ahead)

    share_s.wait_recv()
    both = sums[...] + rsums[...]
    n_q = out.shape[2]
    qi = lax.broadcasted_iota(jnp.int32, (both.shape[1], n_q), 0)
    qj = lax.broadcasted_iota(jnp.int32, (both.shape[1], n_q), 1)
    pick = ((qi >= qj * RANK) & (qi < (qj + 1) * RANK)).astype(jnp.float32)
    scores = jnp.dot(
        both, pick, preferred_element_type=jnp.float32, precision=lax.Precision.HIGHEST
    )
    out[0] = scores[: out.shape[1]]

    share_a.wait_send()
    share_s.wait_send()

    @pl.when(inner)
    def _():
        all_sent(0, pieces, ahead)
        all_sent(1, keep, behind)
        all_sent(2, pieces, behind)
        all_sent(3, pieces, ahead)
        all_sent(4, pieces, behind)
        share_x.wait_send()
        give_back().wait_send()


def on_line(acts, grads, query_left, query_right, seq_len):
    rows, cols = acts.shape[1], query_left.shape[2]
    left_rows, right_rows = query_left.shape[1], query_right.shape[1]
    pieces = (left_rows + right_rows) // T
    dma, f32, bf16 = pltpu.SemaphoreType.DMA, jnp.float32, jnp.bfloat16
    anywhere = pl.BlockSpec(memory_space=pltpu.HBM)
    return pl.pallas_call(
        functools.partial(line_kernel, left_rows, right_rows),
        out_shape=pltpu.VMEM((1, seq_len.shape[0], cols // RANK), f32),
        in_specs=[anywhere] * 5,
        out_specs=pl.BlockSpec(memory_space=pltpu.VMEM),
        scratch_shapes=[
            pltpu.VMEM((rows, acts.shape[2] + grads.shape[2]), bf16),
            pltpu.VMEM((4 * (left_rows + right_rows), cols), bf16),
            pltpu.VMEM((rows, OFF * T), bf16),
            pltpu.VMEM((2, rows, cols), f32),
            pltpu.VMEM((rows, cols), f32),
            pltpu.VMEM((rows, cols), f32),
            pltpu.VMEM((rows, cols), f32),
            pltpu.VMEM((rows, cols), f32),
            pltpu.VMEM((8, cols), f32),
            pltpu.VMEM((8, cols), f32),
            pltpu.VMEM((8, cols), f32),
            pltpu.VMEM((8, cols), f32),
            pltpu.SMEM((seq_len.shape[0],), jnp.int32),
            dma((5,)),
            dma((5,)),
            dma((LATE + 1,)),
            dma((3 * pieces,)),
            dma((LATE + 1,)),
            dma((5,)),
            dma((5,)),
        ],
        compiler_params=pltpu.CompilerParams(
            collective_id=0, has_side_effects=True, vmem_limit_bytes=60 * 1024 * 1024
        ),
    )(acts, grads, query_left, query_right, seq_len)


def fits_line(mesh, acts, query_left, query_right, seq_len):
    rows = acts.shape[1]
    pieces_g = query_right.shape[1] // T
    return (
        mesh.shape["dp"] == 4
        and mesh.shape["mp"] == 2
        and seq_len.shape[0] == 2
        and rows % 32 == 0
        and query_left.shape[1] % T == 0
        and query_right.shape[1] % T == 0
        and query_left.shape[1] >= T
        and pieces_g >= OFF
    )


def solution(mesh):
    def body(acts, grads, query_left, query_right, seq_len):
        if fits_line(mesh, acts, query_left, query_right, seq_len):
            summed = on_line(acts, grads, query_left, query_right, seq_len)
            return summed / math.sqrt(RANK * LEN)
        return on_device(acts, grads, query_left, query_right, seq_len)

    return jax.shard_map(
        body,
        mesh=mesh,
        in_specs=(
            P("layer", ("groups", "dp"), "mp"),
            P("layer", ("groups", "dp"), "mp"),
            P("layer", ("mp", "dp"), "groups"),
            P("layer", ("mp", "dp"), "groups"),
            P(("groups", "dp")),
        ),
        out_specs=P("layer", ("groups", "dp"), None),
        check_vma=False,
    )
```
